32 devices in a mesh: seq: 32 (over z, y, x, core), head: 1.
Axes of the slice: x: 2, y: 2, z: 4, core: 2. Of those that a mesh axis runs over, the one named last changes fastest.
Arguments:
- video_query: bfloat16 [65536, 2048], P('seq', 'head'), may hold values from -360 to 360
- video_kv: bfloat16 [2, 65536, 2048], P(None, 'seq', 'head'), may hold values from -360 to 360
- video_clip: int32 [65536], P('seq'), may hold values from 0 to 7, never falling along the last dimension, each value on 1 to 49152 neighbouring positions
- audio_hidden: bfloat16 [256, 2048], replicated, may hold values from -6 to 6
- audio_qkv_weight: bfloat16 [32, 128, 3072], P('seq', None, 'head'), may hold values from -0.125 to 0.125
- audio_clip: int32 [256], replicated, may hold values from 0 to 7, never falling along the last dimension, each value on 1 to 192 neighbouring positions
- audio_out_weight: bfloat16 [2048, 2048], P('head', 'seq'), may hold values from -0.125 to 0.125
Outputs:
- video_attn: bfloat16 [65536, 2048], P('seq', 'head')
- audio_out: bfloat16 [256, 2048], P('head', 'seq')
The draws below stay inside these ranges and needn't reach their ends.
Inputs may be any that keep to these rules, and one draw needn't show every extreme that they name: `video_clip`: rows of one clip are consecutive; every clip number appears among the video rows. `audio_clip`: rows of one clip are consecutive; every clip number appears among the audio rows.
All inputs are finite; a program needn't handle non-finite values.
Results may differ from the reference program's by a relative error of at most 0.009.
The reference program's roundings to bfloat16 on the way count: a program that leaves them out, or rounds other values in their place, can miss the bound.
Values may be sent and summed in bfloat16 or wider, within the bound.
No kernel may reach another device: no remote copies, remote signals or barrier semaphores. Data moves between devices by JAX's collectives and lax.ppermute only.
A program may use at most 128 MiB of HBM per device.

```python
import math
import jax
import jax.numpy as jnp
import numpy as np
from jax import lax

H = 32
HD = 64
DA = 2048
NA = 256
VTOK_DEV = 2048
CLIPS = 8
NV = 65536
N_SEQ = 32
N_HEAD = 1


def scaled_rows(key, shape):
    key_base = jax.random.fold_in(key, 0)
    base = jnp.clip(jax.random.normal(key_base, shape, jnp.float32), -6.0, 6.0)
    return base


def draw_video_query(key, part):
    values = scaled_rows(jax.random.fold_in(key, 11), (NV, H * HD))
    return values.astype(jnp.bfloat16)


def draw_video_kv(key, part):
    keys = scaled_rows(jax.random.fold_in(key, 23), (NV, H * HD))
    noise = jnp.clip(jax.random.normal(jax.random.fold_in(key, 29), (NV // VTOK_DEV, VTOK_DEV, H * HD), jnp.float32), -6.0, 6.0)
    offsets = 3.0 * jnp.clip(jax.random.normal(jax.random.fold_in(key, 31), (NV // VTOK_DEV, 1, H * HD), jnp.float32), -5.0, 5.0)
    values = (noise + offsets).reshape(NV, H * HD)
    return jnp.stack([keys, values]).astype(jnp.bfloat16)


def level_of(rng, dims, pieces, low, largest):
    def one(dim, shards_of):
        steps = jax.random.uniform(jax.random.fold_in(jax.random.fold_in(rng, 6), dim), (shards_of,), jnp.float32, low / len(pieces), largest / len(pieces))
        return jnp.repeat(jnp.exp(steps), dims[dim] // shards_of).reshape((-1,) + (1,) * (len(dims) - dim - 1))

    loudness = one(*pieces[0])
    for cut in pieces[1:]:
        loudness = loudness * one(*cut)
    return loudness


def length_profile(number_of, total, bound, skew):
    portions = [(1 << 20) // math.isqrt(grade ** skew) + 1 for grade in range(2, number_of + 1)]
    surplus, counts = total - bound - (number_of - 1), [1] * (number_of - 1)
    while surplus > 0:
        free = [i for i in range(number_of - 1) if counts[i] < bound]
        pool, budget = sum([portions[i] for i in free]), surplus
        for i in free:
            addition = min(bound - counts[i], max(1, budget * portions[i] // pool), surplus)
            counts[i] = counts[i] + addition
            surplus = surplus - addition
    return np.array([bound] + counts)


def ragged_sizes(rng, number_of, total, reach, slope):
    if number_of == 2:
        one = jax.random.randint(rng, (), max(1, total - reach), min(reach, total - 1) + 1)
        return jnp.stack([one, total - one])
    tallies = jnp.asarray(length_profile(number_of, total, reach, slope), jnp.int32)
    pairs = (number_of - 1) // 2
    giver, taker = tallies[1:1 + 2 * pairs:2], tallies[2:2 + 2 * pairs:2]
    margin = jnp.minimum(giver - 1, reach - taker)
    moved = jax.random.randint(jax.random.fold_in(rng, 1), (pairs,), 0, 1 << 20) % (margin + 1)
    tallies = tallies.at[1:1 + 2 * pairs:2].set(giver - moved).at[2:2 + 2 * pairs:2].set(taker + moved)
    return tallies[jax.random.permutation(jax.random.fold_in(rng, 2), number_of)]


def scatter_about(rng, dims, deviation, most, shards=(), held_as=jnp.bfloat16):
    values = jax.random.normal(rng, dims, jnp.float32) * deviation
    if len(shards) > 0:
        values = level_of(rng, dims, shards, -0.22, 0.18) * values
    return jnp.clip(values, min=-most, max=most).astype(held_as)


def setup_inputs(seed: int = 0) -> dict:
    streams_of = jax.random.split(jax.random.key(seed), 8)
    video_query = draw_video_query(jax.random.fold_in(streams_of[7], 71), 0)
    video_kv = draw_video_kv(jax.random.fold_in(streams_of[7], 71), 0)
    video_clip = jnp.searchsorted(jnp.cumsum(ragged_sizes(streams_of[2], CLIPS, NV, NV * 3 // 4, 2)), jnp.arange(NV), side="right").astype(jnp.int32)
    audio_hidden = scatter_about(streams_of[3], (NA, DA), 1.0, 6.0)
    audio_qkv_weight = scatter_about(streams_of[4], (N_SEQ, DA // 16, 3 * H * HD * 16 // N_SEQ), DA ** -0.5, 0.125, ((0, 32),))
    audio_clip = jnp.searchsorted(jnp.cumsum(ragged_sizes(streams_of[5], CLIPS, NA, NA * 3 // 4, 2)), jnp.arange(NA), side="right").astype(jnp.int32)
    audio_out_weight = scatter_about(streams_of[6], (H * HD, DA), (H * HD) ** -0.5, 0.125, ((1, 32),))
    return dict(video_query=video_query, video_kv=video_kv, video_clip=video_clip, audio_hidden=audio_hidden, audio_qkv_weight=audio_qkv_weight, audio_clip=audio_clip, audio_out_weight=audio_out_weight)


NEG = -1e30


def video_head(inputs, same):
    query, key, value = inputs
    scores = jnp.dot(query, key.T, preferred_element_type=jnp.float32) * 0.125
    scores = jnp.where(same, scores, NEG)
    top = jnp.max(scores, axis=1, keepdims=True)
    expo = jnp.exp(scores - top)
    probs = (expo / jnp.sum(expo, axis=1, keepdims=True)).astype(jnp.bfloat16)
    return jnp.dot(probs, value, preferred_element_type=jnp.float32)


def audio_head(inputs, same_t):
    query, key, value = inputs
    scores = jnp.dot(query, key.T, preferred_element_type=jnp.float32) * 0.125
    scores = jnp.where(same_t, scores, NEG)
    top = jnp.max(scores, axis=1, keepdims=True)
    weights = jnp.where(same_t, jnp.exp(scores - top), jnp.float32(0.0))
    denominator = jnp.sum(weights, axis=1, keepdims=True)
    numerator = jnp.dot(weights.astype(jnp.bfloat16), value, preferred_element_type=jnp.float32)
    return numerator / denominator


def reference(video_query, video_kv, video_clip, audio_hidden, audio_qkv_weight, audio_clip, audio_out_weight):
    quarters = N_SEQ // 16
    group_heads = H // N_HEAD
    columns = 3 * group_heads * HD // quarters
    laid = audio_qkv_weight.reshape(quarters, 16, DA // 16, N_HEAD, columns)
    laid = jnp.transpose(laid, (1, 2, 3, 0, 4)).reshape(DA, N_HEAD, 3, group_heads, HD)
    flat_weight = jnp.transpose(laid, (0, 2, 1, 3, 4)).reshape(DA, 3 * H * HD)
    audio_qkv = jnp.dot(audio_hidden, flat_weight, preferred_element_type=jnp.float32).astype(jnp.bfloat16)
    audio_qkv = audio_qkv.reshape(NA, 3, H, HD)
    audio_q = jnp.transpose(audio_qkv[:, 0], (1, 0, 2))
    audio_k = jnp.transpose(audio_qkv[:, 1], (1, 0, 2))
    audio_v = jnp.transpose(audio_qkv[:, 2], (1, 0, 2))
    vid_q = jnp.transpose(video_query.reshape(NV, H, HD), (1, 0, 2))
    vid_k = jnp.transpose(video_kv[0].reshape(NV, H, HD), (1, 0, 2))
    vid_v = jnp.transpose(video_kv[1].reshape(NV, H, HD), (1, 0, 2))
    same = video_clip[:, None] == audio_clip[None, :]
    same_t = audio_clip[:, None] == video_clip[None, :]
    video_out = lax.map(lambda item: video_head(item, same), (vid_q, audio_k, audio_v))
    video_attn = jnp.transpose(video_out, (1, 0, 2)).reshape(NV, H * HD).astype(jnp.bfloat16)
    audio_res = lax.map(lambda item: audio_head(item, same_t), (audio_q, vid_k, vid_v))
    audio_attn = jnp.transpose(audio_res, (1, 0, 2)).reshape(NA, H * HD).astype(jnp.bfloat16)
    audio_out = jnp.dot(audio_attn, audio_out_weight, preferred_element_type=jnp.float32).astype(jnp.bfloat16)
    return video_attn, audio_out
```

```python
import functools

import jax
import jax.numpy as jnp
from jax import lax
from jax.experimental import pallas as pl
from jax.experimental.pallas import tpu as pltpu
from jax.sharding import PartitionSpec as P

HD = 64
PAIR = 2 * HD
GROUP = 16
NEG = -1e30
NT = (((1,), (1,)), ((), ()))
SMEM = pl.BlockSpec(memory_space=pltpu.SMEM)


def pick_kernel(where_ref, weight_ref, out_ref):
    members, _, features = out_ref.shape
    quarter = where_ref[0]
    wide = weight_ref.shape[1] // PAIR * 2 // 3
    wide_start = quarter * (wide // 2)
    keys_start = (1 - quarter) * wide
    for member in range(members):
        lanes = pl.ds(pl.multiple_of((wide_start + member) * PAIR, PAIR), PAIR)
        out_ref[member, :PAIR, :] = weight_ref[:, lanes].T
    for two in range(members // 2):
        lanes = pl.ds(pl.multiple_of((keys_start + two) * PAIR, PAIR), PAIR)
        keys = weight_ref[:, lanes].T
        out_ref[2 * two, PAIR:, :] = keys[:HD]
        out_ref[2 * two + 1, PAIR:, :] = keys[HD:]


def project_kernel(weight_ref, hidden_ref, out_ref):
    members, _, features = weight_ref.shape
    total = None
    for member in range(members):
        part = lax.dot_general(
            weight_ref[member],
            hidden_ref[:, member * features : (member + 1) * features],
            NT,
            preferred_element_type=jnp.float32,
        )
        total = part if total is None else total + part
    out_ref[...] = total.astype(out_ref.dtype)


def fill_bias(bias_ref, audio_clip_ref, video_clip_ref):
    bias_ref[...] = jnp.where(
        audio_clip_ref[...] == video_clip_ref[...], jnp.float32(0.0), jnp.float32(NEG)
    )


def audio_kernel(
    table_ref, video_clip_ref, audio_clip_ref, qkv_ref, key_ref, value_ref,
    send_ref, keep_ref, bias_ref, values_ref, *, pairs
):
    step = pl.program_id(0)
    half = send_ref.shape[0]
    width = pairs * PAIR

    @pl.when(step == 0)
    def _():
        fill_bias(bias_ref, audio_clip_ref, video_clip_ref)
        values_ref[:, PAIR:] = jnp.ones((values_ref.shape[0], PAIR), values_ref.dtype)
        send_ref[:, width:] = jnp.zeros((half, PAIR), jnp.float32)
        keep_ref[:, width:] = jnp.zeros((half, PAIR), jnp.float32)

    values_ref[:, :PAIR] = value_ref[0]
    first = pl.multiple_of(table_ref[step], HD)
    query = qkv_ref[pl.ds(first, PAIR), :] * jnp.bfloat16(0.125)
    row = lax.broadcasted_iota(jnp.int32, query.shape, 0)
    lane = lax.broadcasted_iota(jnp.int32, (2 * half, PAIR), 1)
    outs, stats = [], None
    for h in range(2):
        own = (row >= HD) if h else (row < HD)
        query_h = jnp.where(own, query, jnp.zeros_like(query)).T
        scores = lax.dot_general(query_h, key_ref[0], NT, preferred_element_type=jnp.float32)
        scores = scores + bias_ref[...]
        top = jnp.max(scores, axis=1, keepdims=True)
        weights = jnp.exp(scores - top).astype(jnp.bfloat16)
        out = jnp.dot(weights, values_ref[...], preferred_element_type=jnp.float32)
        outs.append(out[:, :PAIR])
        head = 2 * step + h
        mine = jnp.where(lane == head, top, jnp.where(lane == head + HD, out[:, PAIR:], 0.0))
        stats = mine if stats is None else stats + mine
    numer = jnp.where(lane < HD, outs[0], outs[1])
    lanes = pl.ds(pl.multiple_of(step * PAIR, PAIR), PAIR)
    upper = table_ref[4 * pairs] == 1
    keep_ref[:, lanes] = jnp.where(upper, numer[half:], numer[:half])
    send_ref[:, lanes] = jnp.where(upper, numer[:half], numer[half:])
    keep_ref[:, width:] += jnp.where(upper, stats[half:], stats[:half])
    send_ref[:, width:] += jnp.where(upper, stats[:half], stats[half:])


def audio_partials(table, video_clip, audio_clip, qkv, video_kv):
    rows = qkv.shape[1]
    _, length, width = video_kv.shape
    pairs = width // PAIR
    half = jax.ShapeDtypeStruct((rows // 2, width + PAIR), jnp.float32)
    half_spec = pl.BlockSpec((rows // 2, width + PAIR), lambda p, t: (0, 0))
    return pl.pallas_call(
        functools.partial(audio_kernel, pairs=pairs),
        grid_spec=pltpu.PrefetchScalarGridSpec(
            num_scalar_prefetch=1,
            grid=(pairs,),
            in_specs=[
                pl.BlockSpec((1, length), lambda p, t: (0, 0)),
                pl.BlockSpec((rows, 1), lambda p, t: (0, 0)),
                pl.BlockSpec(qkv.shape, lambda p, t: (0, 0)),
                pl.BlockSpec((1, length, PAIR), lambda p, t: (0, 0, p)),
                pl.BlockSpec((1, length, PAIR), lambda p, t: (1, 0, p)),
            ],
            out_specs=[half_spec, half_spec],
            scratch_shapes=[
                pltpu.VMEM((rows, length), jnp.float32),
                pltpu.VMEM((length, 2 * PAIR), jnp.bfloat16),
            ],
        ),
        out_shape=[half, half],
        name="audio_partials",
    )(table, video_clip, audio_clip, qkv, video_kv, video_kv)


def video_kernel(
    table_ref, video_clip_ref, audio_clip_ref, qkv_ref, query_ref, out_ref, bias_ref,
    *, pairs, block
):
    step = pl.program_id(0)
    rows = qkv_ref.shape[1]

    @pl.when(step == 0)
    def _():
        fill_bias(bias_ref, audio_clip_ref, video_clip_ref)

    value_start = pl.multiple_of(table_ref[3 * pairs + step], HD)
    blank = jnp.zeros((HD, rows), jnp.bfloat16)
    ones = jnp.ones((16, rows), jnp.bfloat16)
    keys, values = [], []
    for h in range(2):
        key_start = pl.multiple_of(table_ref[pairs + 2 * step + h], HD)
        key = qkv_ref[pl.ds(key_start, HD), :] * jnp.bfloat16(0.125)
        keys.append(jnp.concatenate([blank, key] if h else [key, blank], axis=0).T)
        value = qkv_ref[pl.ds(value_start + h * HD, HD), :]
        values.append(jnp.concatenate([value, ones], axis=0))
    for start in range(0, query_ref.shape[0], block):
        columns = slice(start, start + block)
        outs = []
        for h in range(2):
            scores = lax.dot_general(
                keys[h], query_ref[columns, :], NT, preferred_element_type=jnp.float32
            )
            scores = scores + bias_ref[:, columns]
            top = jnp.max(scores, axis=0, keepdims=True)
            weights = jnp.exp(scores - top).astype(jnp.bfloat16)
            out = jnp.dot(values[h], weights, preferred_element_type=jnp.float32)
            outs.append(out[:HD] * (1.0 / out[HD : HD + 1]))
        out_ref[columns, :] = jnp.concatenate(outs, axis=0).T.astype(out_ref.dtype)


def video_attend(table, video_clip, audio_clip, qkv, video_query, block=512):
    rows = qkv.shape[1]
    length, width = video_query.shape
    pairs = width // PAIR
    return pl.pallas_call(
        functools.partial(video_kernel, pairs=pairs, block=block),
        grid_spec=pltpu.PrefetchScalarGridSpec(
            num_scalar_prefetch=1,
            grid=(pairs,),
            in_specs=[
                pl.BlockSpec((1, length), lambda p, t: (0, 0)),
                pl.BlockSpec((rows, 1), lambda p, t: (0, 0)),
                pl.BlockSpec(qkv.shape, lambda p, t: (0, 0)),
                pl.BlockSpec((length, PAIR), lambda p, t: (0, p)),
            ],
            out_specs=pl.BlockSpec((length, PAIR), lambda p, t: (0, p)),
            scratch_shapes=[pltpu.VMEM((rows, length), jnp.float32)],
        ),
        out_shape=jax.ShapeDtypeStruct((length, width), jnp.bfloat16),
        name="video_attend",
    )(table, video_clip, audio_clip, qkv, video_query)


def merged(keep_ref, other_ref, rows, width):
    mine, theirs = keep_ref[rows, width:], other_ref[rows, width:]
    top = jnp.maximum(mine, theirs)
    mine_by, theirs_by = jnp.exp(mine - top), jnp.exp(theirs - top)
    total = mine * pltpu.roll(mine_by, HD, 1) + theirs * pltpu.roll(theirs_by, HD, 1)
    lane = lax.broadcasted_iota(jnp.int32, top.shape, 1)
    stats = jnp.where(lane < HD, top, total)

    def numerator(pair):
        lanes = slice(pair * PAIR, (pair + 1) * PAIR)

        def spread(by):
            two = slice(2 * pair, 2 * pair + 1), slice(2 * pair + 1, 2 * pair + 2)
            return jnp.where(lane < HD, by[:, two[0]], by[:, two[1]])

        return keep_ref[rows, lanes] * spread(mine_by) + other_ref[rows, lanes] * spread(theirs_by)

    return numerator, stats


def merge_kernel(bit_ref, keep_ref, other_ref, send_ref, next_ref):
    half, width = send_ref.shape[0], send_ref.shape[1] - PAIR
    bit = bit_ref[0]
    for out_ref, part in ((send_ref, 1 - bit), (next_ref, bit)):
        rows = pl.ds(pl.multiple_of(part * half, half), half)
        numerator, stats = merged(keep_ref, other_ref, rows, width)
        for pair in range(width // PAIR):
            out_ref[:, pair * PAIR : (pair + 1) * PAIR] = numerator(pair)
        out_ref[:, width:] = stats


def finish_kernel(keep_ref, other_ref, out_ref):
    width = out_ref.shape[1]
    numerator, stats = merged(keep_ref, other_ref, slice(None), width)
    lane = lax.broadcasted_iota(jnp.int32, stats.shape, 1)
    for pair in range(width // PAIR):
        first = HD + 2 * pair
        total = jnp.where(lane < HD, stats[:, first : first + 1], stats[:, first + 1 : first + 2])
        out_ref[:, pair * PAIR : (pair + 1) * PAIR] = (numerator(pair) / total).astype(out_ref.dtype)


def mirrored(index, size):
    result = 0 * index
    for bit in range(size.bit_length() - 1):
        result = 2 * result + index // (1 << bit) % 2
    return result


def out_kernel(position_ref, attn_ref, weight_ref, out_ref, rows_ref, *, size):
    share = attn_ref.shape[0] // size
    position = position_ref[0]
    result = jnp.dot(attn_ref[...], weight_ref[...], preferred_element_type=jnp.float32)
    for block in range(size):
        start, bit, length = 0, 1, attn_ref.shape[0]
        device = position ^ mirrored(block, size)
        while bit < size:
            length //= 2
            start = start + (device // bit % 2) * length
            bit *= 2
        rows_ref[pl.ds(pl.multiple_of(start, share), share), :] = result[
            block * share : (block + 1) * share
        ]
    out_ref[...] = rows_ref[...].astype(out_ref.dtype)


def swap(array, bit, size):
    return lax.ppermute(array, "seq", [(i, i ^ bit) for i in range(size)])


def gathered(array, size):
    bits = [1 << k for k in range(size.bit_length() - 1)]
    ordered = array
    for bit in reversed(bits):
        ordered = jnp.concatenate([ordered[None], swap(ordered, bit, size)[None]], axis=0)
    ordered = ordered.reshape((2,) * len(bits) + array.shape)
    return ordered.reshape((size * array.shape[0],) + array.shape[1:])


def projected_parts(position, audio_hidden, weight, size):
    features, columns = weight.shape
    rows = audio_hidden.shape[0]
    share = columns // GROUP
    picked = pl.pallas_call(
        pick_kernel,
        in_specs=[SMEM, pl.BlockSpec(memory_space=pltpu.VMEM)],
        out_shape=jax.ShapeDtypeStruct((GROUP, share, features), weight.dtype),
        name="pick",
    )((position // GROUP)[None], weight)
    groups = [list(range(s, s + GROUP)) for s in range(0, size, GROUP)]
    own = lax.all_to_all(picked, "seq", 0, 0, axis_index_groups=groups)
    part = pl.pallas_call(
        project_kernel,
        out_shape=jax.ShapeDtypeStruct((share, rows), jnp.bfloat16),
        name="project",
    )(own, audio_hidden)
    qkv = gathered(part, size)
    blocks = mirrored(position ^ jnp.arange(size), size) * share
    return qkv, jnp.concatenate([blocks[:GROUP], blocks + PAIR, blocks[GROUP:]])


def projected_whole(position, audio_hidden, weight, size):
    features, columns = weight.shape
    rows = audio_hidden.shape[0]
    quarters = size // GROUP
    mine = lax.dynamic_slice_in_dim(audio_hidden, position % GROUP * features, features, 1)
    part = jnp.dot(mine, weight, preferred_element_type=jnp.float32)
    padded = jnp.zeros((rows, quarters * columns), jnp.float32)
    placed = lax.dynamic_update_slice_in_dim(padded, part, position // GROUP * columns, 1)
    qkv = lax.psum(placed, "seq").astype(jnp.bfloat16).T
    width = quarters * columns // 3
    queries = jnp.arange(0, width, PAIR)
    keys = jnp.arange(width, 2 * width, HD)
    return qkv, jnp.concatenate([queries, keys, 2 * width + queries])


def finished_rows(position, send, keep, size):
    bit = 1
    while bit < size:
        other = swap(send, bit, size)
        bit *= 2
        shape = (keep.shape[0] // 2, keep.shape[1])
        if bit < size:
            send, keep = pl.pallas_call(
                merge_kernel,
                in_specs=[SMEM] + [pl.BlockSpec(memory_space=pltpu.VMEM)] * 2,
                out_shape=[jax.ShapeDtypeStruct(shape, jnp.float32)] * 2,
                name="merge",
            )((position // bit % 2)[None], keep, other)
    return pl.pallas_call(
        finish_kernel,
        out_shape=jax.ShapeDtypeStruct((keep.shape[0], keep.shape[1] - PAIR), jnp.bfloat16),
        name="finish",
    )(keep, other)


def whole_rows(position, send, keep, size):
    first = position % 2 == 0
    both = jnp.where(
        first, jnp.concatenate([keep, send], axis=0), jnp.concatenate([send, keep], axis=0)
    )
    width = both.shape[1] - PAIR
    heads = width // HD
    numer = both[:, :width].reshape(-1, heads, HD)
    top, total = both[:, width : width + heads], both[:, width + HD : width + HD + heads]
    factor = jnp.exp(top - lax.pmax(top, "seq"))
    numer = lax.psum_scatter(
        (numer * factor[:, :, None]).reshape(-1, width), "seq", scatter_dimension=0, tiled=True
    )
    total = lax.psum_scatter(total * factor, "seq", scatter_dimension=0, tiled=True)
    done = (numer.reshape(-1, heads, HD) / total[:, :, None]).reshape(-1, width)
    return lax.all_gather(done.astype(jnp.bfloat16), "seq", axis=0, tiled=True)


def shards(
    video_query, video_kv, video_clip, audio_hidden, audio_qkv_weight, audio_clip, audio_out_weight
):
    size = lax.axis_size("seq")
    position = lax.axis_index("seq")
    rows = audio_hidden.shape[0]
    width = video_query.shape[1]
    pairs = width // PAIR
    halves = size == 2 * GROUP and pairs == GROUP
    project = projected_parts if halves else projected_whole
    qkv, starts = project(position, audio_hidden, audio_qkv_weight[0], size)
    table = jnp.concatenate([starts, (position % 2)[None]]).astype(jnp.int32)
    clips = video_clip[None], audio_clip[:, None]
    send, keep = audio_partials(table, *clips, qkv, video_kv)
    video_attn = video_attend(table, *clips, qkv, video_query)
    if rows % (8 * size) == 0 and lax.axis_size("head") == 1:
        attn = gathered(finished_rows(position, send, keep, size), size)
        audio_out = pl.pallas_call(
            functools.partial(out_kernel, size=size),
            in_specs=[SMEM] + [pl.BlockSpec(memory_space=pltpu.VMEM)] * 2,
            out_shape=jax.ShapeDtypeStruct((rows, audio_out_weight.shape[1]), jnp.bfloat16),
            scratch_shapes=[pltpu.VMEM((rows, audio_out_weight.shape[1]), jnp.float32)],
            name="out",
        )(position[None], attn, audio_out_weight)
        return video_attn, audio_out
    attn = whole_rows(position, send, keep, size)
    audio_out = lax.psum_scatter(
        jnp.dot(attn, audio_out_weight, preferred_element_type=jnp.float32),
        "head",
        scatter_dimension=0,
        tiled=True,
    )
    return video_attn, audio_out.astype(jnp.bfloat16)


def solution(mesh):
    return jax.shard_map(
        shards,
        mesh=mesh,
        in_specs=(
            P("seq", "head"),
            P(None, "seq", "head"),
            P("seq"),
            P(),
            P("seq", None, "head"),
            P(),
            P("head", "seq"),
        ),
        out_specs=(P("seq", "head"), P("head", "seq")),
        check_vma=False,
    )
```
